32 devices in a mesh: lat: 4 (over z), fld: 4 (over y, x), rep: 2 (over core).
Axes of the slice: x: 2, y: 2, z: 4, core: 2. Of those that a mesh axis runs over, the one named last changes fastest.
Arguments:
- field: float32 [12, 1280, 2560], P('fld', ('lat', 'rep')), may hold values from -6 to 6
- wind_zonal: float32 [12, 1280, 2560], P('fld', ('lat', 'rep')), may hold values from -4 to 4
- wind_merid: float32 [12, 1280, 2560], P('fld', ('lat', 'rep')), may hold values from -4 to 4
- band: int32 [12, 2], replicated, may hold values from 0 to 1280, as said below
- waves: int32 [16, 80], replicated, may hold values from -1 to 1279, as said below
- legendre: bfloat16 [16, 1280, 51328], P(('lat', 'fld')), may hold values from -0.15625 to 0.15625
Outputs:
- spectrum: float32 [16, 12, 2, 51328], P(('lat', 'fld'), 'rep')
The draws below stay inside these ranges and needn't reach their ends.
Inputs may be any that keep to these rules, and one draw needn't show every extreme that they name: band[f, 0] is below 320 and band[f, 1] is above 960, for every field-level. `waves`: every wavenumber 0 to 1279 stands in exactly one slot of one group; -1 marks an empty slot. Wavenumber m takes 1280 - m columns, and the wavenumbers of one group take at most 51240 columns together; some group takes exactly 51240.
All inputs are finite; a program needn't handle non-finite values.
Results may differ from the reference program's by a relative error of at most 0.0056.
Values may be sent and summed in bfloat16 or wider, within the bound.
A program may use at most 256 MiB of HBM per device.

```python
import math
import jax
import jax.numpy as jnp
from jax import lax

NLAT = 1280
NLON = 2560
M = 1280
F = 12
GROUPS = 16
ROUNDS = 40
REST = 0
SLOTS = 80
COLS = 51328


def draw_band(key, part):
    keys = jax.random.split(jax.random.fold_in(key, 11), 4)
    quarter = NLAT // 4
    lower_rows = jax.random.randint(keys[0], (F,), 0, quarter)
    upper_rows = NLAT - jax.random.randint(keys[1], (F,), 0, quarter)
    lower_rows = lower_rows.at[jax.random.randint(keys[2], (), 0, F)].set(0)
    upper_rows = upper_rows.at[jax.random.randint(keys[3], (), 0, F)].set(NLAT)
    return jnp.stack([lower_rows, upper_rows], axis=1).astype(jnp.int32)


def draw_waves(key, part):
    base_key = jax.random.fold_in(key, 23)
    assignment = -jnp.ones((GROUPS, SLOTS), jnp.int32)
    positions = jnp.arange(GROUPS, dtype=jnp.int32)
    for round_index in range(ROUNDS):
        ordering = jax.random.permutation(jax.random.fold_in(base_key, round_index), GROUPS)
        first_waves = 2 * round_index * GROUPS + positions
        second_waves = (2 * round_index + 2) * GROUPS - 1 - positions
        assignment = assignment.at[ordering, 2 * round_index].set(first_waves)
        assignment = assignment.at[ordering, 2 * round_index + 1].set(second_waves)
    if REST > 0:
        ordering = jax.random.permutation(jax.random.fold_in(base_key, ROUNDS + 7), GROUPS)
        rest_waves = jnp.where(positions < REST, 2 * ROUNDS * GROUPS + positions, -1).astype(jnp.int32)
        assignment = assignment.at[ordering, 2 * ROUNDS].set(rest_waves)
    slot_scores = jax.random.randint(jax.random.fold_in(base_key, 5003), (GROUPS, SLOTS), 0, 1 << 20)
    slot_scores = slot_scores * SLOTS + jnp.arange(SLOTS, dtype=jnp.int32)[None, :]
    shuffle = jnp.argsort(slot_scores, axis=1)
    return jnp.take_along_axis(assignment, shuffle, axis=1).astype(jnp.int32)


def block_levels(key, shape, cuts, low, largest):
    def one(position, blocks):
        heights = jax.random.uniform(jax.random.fold_in(jax.random.fold_in(key, 6), position), (blocks,), jnp.float32, low / len(cuts), largest / len(cuts))
        return jnp.repeat(jnp.exp(heights), shape[position] // blocks).reshape((-1,) + (1,) * (len(shape) - position - 1))

    loudness = one(*cuts[0])
    for cut in cuts[1:]:
        loudness = loudness * one(*cut)
    return loudness


def scatter_about(stream_key, dims, scale, limit, shards=(), held_as=jnp.bfloat16):
    drawn = jax.random.normal(stream_key, dims, jnp.float32) * scale
    if len(shards) > 0:
        drawn = block_levels(stream_key, dims, shards, -0.22, 0.18) * drawn
    return jnp.clip(drawn, min=-limit, max=limit).astype(held_as)


def setup_inputs(seed: int = 0) -> dict:
    seeds = jax.random.split(jax.random.key(seed), 7)
    field = scatter_about(seeds[0], (F, NLAT, NLON), 1.0, 6.0, ((0, 4), (1, 8)), jnp.float32)
    wind_zonal = scatter_about(seeds[1], (F, NLAT, NLON), 1.0, 4.0, ((0, 4), (1, 8)), jnp.float32)
    wind_merid = scatter_about(seeds[2], (F, NLAT, NLON), 1.0, 4.0, ((0, 4), (1, 8)), jnp.float32)
    band = draw_band(jax.random.fold_in(seeds[6], 71), 0)
    waves = draw_waves(jax.random.fold_in(seeds[6], 71), 0)
    legendre = scatter_about(seeds[5], (GROUPS, NLAT, COLS), NLAT ** -0.5, 0.15625, ((0, 16),))
    return {"field": field, "wind_zonal": wind_zonal, "wind_merid": wind_merid, "band": band, "waves": waves, "legendre": legendre}


def dft_matrix(lon_count, wave_count):
    lon_ids = lax.broadcasted_iota(jnp.int32, (lon_count, wave_count), 0)
    wave_ids = lax.broadcasted_iota(jnp.int32, (lon_count, wave_count), 1)
    angles = (lon_ids * wave_ids % lon_count).astype(jnp.float32) * (2.0 * math.pi / lon_count)
    scaling = 1.0 / math.sqrt(lon_count)
    return jnp.concatenate([jnp.cos(angles) * scaling, -jnp.sin(angles) * scaling], axis=1).astype(jnp.bfloat16)

def tendency(centre, above_row, below_row, zonal_wind, merid_wind):
    eastward = jnp.roll(centre, -1, axis=-1)
    westward = jnp.roll(centre, 1, axis=-1)
    return -(zonal_wind + centre) * (eastward - westward) * 0.5 - merid_wind * (above_row - below_row) * 0.5

def reference(field, wind_zonal, wind_merid, band, waves, legendre):
    matrix = dft_matrix(NLON, M)
    row_ids = jnp.arange(NLAT).astype(jnp.int32)[:, None]

    def one_field(inputs):
        values, zonal_wind, merid_wind, bounds = inputs
        in_band = ((row_ids >= bounds[0]) & (row_ids < bounds[1])).astype(jnp.float32)
        padded = jnp.pad(values, ((1, 1), (0, 0)))
        first_section = values + in_band * tendency(values, padded[2:], padded[:-2], zonal_wind, merid_wind)
        padded_section = jnp.pad(first_section, ((1, 1), (0, 0)))
        advected = 0.5 * (values + first_section + in_band * tendency(first_section, padded_section[2:], padded_section[:-2], zonal_wind, merid_wind))
        grid_low = advected.astype(jnp.bfloat16)
        return jnp.dot(grid_low, matrix, preferred_element_type=jnp.float32).astype(jnp.bfloat16)
    spectra = lax.map(one_field, (field, wind_zonal, wind_merid, band))
    spectra = spectra.reshape(F, NLAT, 2, M)
    col_ids = jnp.arange(COLS).astype(jnp.int32)

    def one_group(inputs):
        own_waves, columns = inputs
        own_filled = own_waves >= 0
        wave_index = jnp.where(own_filled, own_waves, 0).astype(jnp.int32)
        counts = jnp.where(own_filled, M - own_waves, 0).astype(jnp.int32)
        offsets = (jnp.cumsum(counts) - counts).astype(jnp.int32)
        segments = ((col_ids[None, :] >= offsets[:, None]) & (col_ids[None, :] < (offsets + counts)[:, None])).astype(jnp.float32)
        picked = jnp.take(spectra, wave_index, axis=3).astype(jnp.float32)
        products = jnp.einsum('flcs,lk->sfck', picked, columns.astype(jnp.float32))
        return jnp.einsum('sfck,sk->fck', products, segments)
    return lax.map(one_group, (waves, legendre))
```

```python
import functools
import math

import jax
import jax.numpy as jnp
from jax import lax
from jax.experimental import pallas as pl
from jax.experimental.pallas import tpu as pltpu
from jax.sharding import PartitionSpec as P

M = 1280
LANES = 128
WINDOW = 16
TILE = 1024


def with_halo(value, sides, width):
    for axis, dim in sides:
        peers, length = (lax.axis_size(axis), value.shape[dim])
        up = [(i, (i + 1) % peers) for i in range(peers - 1)]
        down = [(j, i) for i, j in up]
        last = lax.slice_in_dim(value, length - width, length, axis=dim)
        first = lax.slice_in_dim(value, 0, width, axis=dim)
        before = lax.ppermute(last, axis, up)
        after = lax.ppermute(first, axis, down)
        value = jnp.concatenate([before, value, after], axis=dim)
    return value


def dft_matrix(lon_count, wave_count):
    lon_ids = lax.broadcasted_iota(jnp.int32, (lon_count, wave_count), 0)
    wave_ids = lax.broadcasted_iota(jnp.int32, (lon_count, wave_count), 1)
    angles = (lon_ids * wave_ids % lon_count).astype(jnp.float32) * (2.0 * math.pi / lon_count)
    scaling = 1.0 / math.sqrt(lon_count)
    return jnp.concatenate([jnp.cos(angles) * scaling, -jnp.sin(angles) * scaling], axis=1).astype(
        jnp.bfloat16
    )


def tendency(centre, above_row, below_row, zonal_wind, merid_wind):
    eastward = jnp.roll(centre, -1, axis=-1)
    westward = jnp.roll(centre, 1, axis=-1)
    return (
        -(zonal_wind + centre) * (eastward - westward) * 0.5
        - merid_wind * (above_row - below_row) * 0.5
    )


def band_mask(bounds, first_row, row_total):
    row_ids = first_row + lax.broadcasted_iota(jnp.int32, (1, row_total, 1), 1)
    lower_edge = bounds[:, 0][:, None, None]
    upper_edge = bounds[:, 1][:, None, None]
    return ((row_ids >= lower_edge) & (row_ids < upper_edge)).astype(jnp.float32)


def transform_kernel(lon_count, table_ref, grid_ref, out_ref, matrix):
    slots = table_ref.shape[1]
    low_cos, low_sin = table_ref[0], table_ref[1]
    high_cos, high_sin = table_ref[2], table_ref[3]
    for part in range(lon_count // LANES):
        columns = slice(part * LANES, (part + 1) * LANES)
        scaled_cos = high_cos[:, part : part + 1]
        scaled_sin = high_sin[:, part : part + 1]
        matrix[0:slots, columns] = (scaled_cos * low_cos - scaled_sin * low_sin).astype(jnp.bfloat16)
        matrix[slots : 2 * slots, columns] = (-(scaled_sin * low_cos + scaled_cos * low_sin)).astype(
            jnp.bfloat16
        )
    out_ref[...] = lax.dot_general(
        matrix[...], grid_ref[...], (((1,), (1,)), ((), ())), preferred_element_type=jnp.float32
    ).astype(jnp.bfloat16)


def transform(grid_low, waves, lon_count):
    groups, slots = waves.shape
    wave_column = jnp.where(waves >= 0, waves, 0).reshape(1, groups * slots, 1)
    step = jnp.arange(2, dtype=jnp.int32).reshape(2, 1, 1) * (LANES - 1) + 1
    lane = lax.broadcasted_iota(jnp.int32, (1, 1, LANES), 2)
    turns = (wave_column * ((step * lane) % lon_count)) % lon_count
    angles = turns.astype(jnp.float32) * (2.0 * math.pi / lon_count)
    scale = jnp.array([1.0, 1.0 / math.sqrt(lon_count)], jnp.float32).reshape(2, 1, 1)
    tables = jnp.stack([jnp.cos(angles) * scale, jnp.sin(angles) * scale], axis=1)
    tables = tables.reshape(4, groups * slots, LANES)
    rows = grid_low.shape[0]
    return pl.pallas_call(
        functools.partial(transform_kernel, lon_count),
        out_shape=jax.ShapeDtypeStruct((groups * 2 * slots, rows), jnp.bfloat16),
        grid=(groups,),
        in_specs=[
            pl.BlockSpec((4, slots, LANES), lambda g: (0, g, 0)),
            pl.BlockSpec((rows, lon_count), lambda g: (0, 0)),
        ],
        out_specs=pl.BlockSpec((2 * slots, rows), lambda g: (g, 0)),
        scratch_shapes=[pltpu.VMEM((2 * slots, lon_count), jnp.bfloat16)],
        compiler_params=pltpu.CompilerParams(vmem_limit_bytes=32 << 20),
    )(tables, grid_low)


def exchange_kernel(lat_size, fld_size, rep_size, source, target, send_sem, recv_sem, own_sem):
    lat, fld, rep = lax.axis_index("lat"), lax.axis_index("fld"), lax.axis_index("rep")
    groups = lat_size * fld_size
    rows = target.shape[1]
    half = fld_size // rep_size
    to_rep = fld // half
    place = ((fld % half) * lat_size + lat) * rep_size + rep
    own = lat * fld_size + fld
    stays = to_rep == rep

    def sending(hop):
        group = (own + hop) % groups
        return pltpu.make_async_remote_copy(
            src_ref=source.at[pl.ds(pl.multiple_of(group * rows, 16), rows)],
            dst_ref=target.at[place],
            send_sem=send_sem.at[hop],
            recv_sem=recv_sem.at[place],
            device_id=(group // fld_size, group % fld_size, to_rep),
            device_id_type=pl.DeviceIdType.MESH,
        )

    kept = pltpu.make_async_copy(
        source.at[pl.ds(pl.multiple_of(own * rows, 16), rows)], target.at[place], own_sem
    )
    for hop in range(1, groups):
        sending(hop).start()

    @pl.when(stays)
    def _():
        kept.start()

    @pl.when(jnp.logical_not(stays))
    def _():
        sending(0).start()

    @pl.when(stays)
    def _():
        kept.wait()

    @pl.when(jnp.logical_not(stays))
    def _():
        sending(0).wait_send()

    for hop in range(1, groups):
        sending(hop).wait_send()
    for origin in range(target.shape[0]):

        @pl.when(jnp.logical_not(stays & (place == origin)))
        def _():
            pltpu.make_async_remote_copy(
                src_ref=target.at[origin],
                dst_ref=target.at[origin],
                send_sem=send_sem.at[0],
                recv_sem=recv_sem.at[origin],
                device_id=(lat, fld, 1 - rep),
                device_id_type=pl.DeviceIdType.MESH,
            ).wait_recv()


def exchange(spectra, lat_size, fld_size, rep_size):
    rows = spectra.shape[0] // (lat_size * fld_size)
    origins = fld_size // rep_size * lat_size * rep_size
    return pl.pallas_call(
        functools.partial(exchange_kernel, lat_size, fld_size, rep_size),
        out_shape=jax.ShapeDtypeStruct((origins, rows, spectra.shape[1]), spectra.dtype),
        in_specs=[pl.BlockSpec(memory_space=pltpu.VMEM)],
        out_specs=pl.BlockSpec(memory_space=pltpu.VMEM),
        scratch_shapes=[
            pltpu.SemaphoreType.DMA((lat_size * fld_size,)),
            pltpu.SemaphoreType.DMA((origins,)),
            pltpu.SemaphoreType.DMA,
        ],
        compiler_params=pltpu.CompilerParams(has_side_effects=True, vmem_limit_bytes=16 << 20),
    )(spectra)


def legendre_kernel(
    bands, field_count, first, last, received, starts, stops, legendre, out, ordered, total
):
    slots = starts.shape[0]
    row_count = received.shape[2] // field_count
    tile = pl.program_id(0)
    width = out.shape[3]

    @pl.when(tile == 0)
    def _():
        for origin in range(received.shape[0]):
            part, band = divmod(origin, bands)
            for level in range(field_count):
                for side in range(2):
                    row = (part * field_count + level) * 2 + side
                    ordered[row, :, band * row_count : (band + 1) * row_count] = received[
                        origin,
                        side * slots : (side + 1) * slots,
                        level * row_count : (level + 1) * row_count,
                    ]

    total[...] = jnp.zeros_like(total)
    rows = ordered.shape[0]

    @pl.loop(first[tile], last[tile])
    def _(window):
        here = pl.ds(pl.multiple_of(window * WINDOW, WINDOW), WINDOW)
        products = jnp.dot(
            ordered[:, here, :].reshape(rows * WINDOW, ordered.shape[2]),
            legendre[0],
            preferred_element_type=jnp.float32,
        ).reshape(rows, WINDOW, width)
        columns = tile * width + lax.broadcasted_iota(jnp.int32, (WINDOW, width), 1)
        held = (columns >= starts[here, :]) & (columns < stops[here, :])
        total[...] += jnp.sum(jnp.where(held[None], products, 0.0), axis=1)

    for level in range(rows // 2):
        out[0, level] = total[2 * level : 2 * level + 2, :]


def legendre_sums(received, own_waves, legendre, field_count, bands, wave_total):
    slots = own_waves.shape[0]
    counts = jnp.where(own_waves >= 0, wave_total - own_waves, 0)
    lower = lax.broadcasted_iota(jnp.int32, (slots, slots), 1) <= lax.broadcasted_iota(
        jnp.int32, (slots, slots), 0
    )
    stops = jnp.sum(jnp.where(lower, counts[None, :], 0), axis=1)
    starts = stops - counts
    depth, col_count = legendre.shape[1:]
    width = min(TILE, col_count)
    tiles = pl.cdiv(col_count, width)
    edges = jnp.arange(tiles, dtype=jnp.int32)[:, None] * width
    first = jnp.sum((stops[None, :] <= edges).astype(jnp.int32), axis=1) // WINDOW
    begun = jnp.sum((starts[None, :] < edges + width).astype(jnp.int32), axis=1)
    last = (begun + WINDOW - 1) // WINDOW
    rows = received.shape[0] // bands * field_count * 2
    return pl.pallas_call(
        functools.partial(legendre_kernel, bands, field_count),
        out_shape=jax.ShapeDtypeStruct((1, rows // 2, 2, col_count), jnp.float32),
        grid_spec=pltpu.PrefetchScalarGridSpec(
            num_scalar_prefetch=2,
            grid=(tiles,),
            in_specs=[
                pl.BlockSpec(
                    received.shape, lambda t, *_: (0, 0, 0), pipeline_mode=pl.Buffered(1)
                ),
                pl.BlockSpec((slots, 1), lambda t, *_: (0, 0)),
                pl.BlockSpec((slots, 1), lambda t, *_: (0, 0)),
                pl.BlockSpec((1, depth, width), lambda t, *_: (0, 0, t)),
            ],
            out_specs=pl.BlockSpec((1, rows // 2, 2, width), lambda t, *_: (0, 0, 0, t)),
            scratch_shapes=[
                pltpu.VMEM((rows, slots, depth), jnp.bfloat16),
                pltpu.VMEM((rows, width), jnp.float32),
            ],
        ),
        compiler_params=pltpu.CompilerParams(vmem_limit_bytes=48 << 20),
    )(first, last, received, starts[:, None], stops[:, None], legendre)


def body(field, wind_zonal, wind_merid, band, waves, legendre):
    field_count, row_count, lon_count = field.shape
    lat_size = lax.axis_size("lat")
    fld_size = lax.axis_size("fld")
    rep_size = lax.axis_size("rep")
    first_row = (lax.axis_index("lat") * rep_size + lax.axis_index("rep")) * row_count
    bounds = lax.dynamic_slice_in_dim(band, lax.axis_index("fld") * field_count, field_count, 0)
    in_band = band_mask(bounds, first_row, row_count)
    padded = with_halo(field, ((("lat", "rep"), 1),), 1)
    first_section = field + in_band * tendency(
        field, padded[:, 2:], padded[:, :-2], wind_zonal, wind_merid
    )
    padded_section = with_halo(first_section, ((("lat", "rep"), 1),), 1)
    advected = 0.5 * (
        field
        + first_section
        + in_band
        * tendency(
            first_section, padded_section[:, 2:], padded_section[:, :-2], wind_zonal, wind_merid
        )
    )
    grid_low = advected.astype(jnp.bfloat16)
    slot_count = waves.shape[1]
    direct = (
        row_count % 16 == 0
        and slot_count % WINDOW == 0
        and lon_count % LANES == 0
        and lon_count // LANES <= LANES
        and fld_size % rep_size == 0
        and lat_size * fld_size <= 64
    )
    if direct:
        spectra = transform(
            grid_low.reshape(field_count * row_count, lon_count), waves, lon_count
        )
        received = exchange(spectra, lat_size, fld_size, rep_size)
        group = lax.axis_index("lat") * fld_size + lax.axis_index("fld")
        own_waves = lax.dynamic_index_in_dim(waves, group, 0, keepdims=False)
        return legendre_sums(
            received, own_waves, legendre, field_count, lat_size * rep_size, M
        )
    spectra = jnp.dot(
        grid_low.reshape(field_count * row_count, lon_count),
        dft_matrix(lon_count, M),
        preferred_element_type=jnp.float32,
    ).astype(jnp.bfloat16)
    spectra = spectra.reshape(field_count, row_count, 2, M)
    wave_index = jnp.where(waves >= 0, waves, 0)
    picked = jnp.take(spectra, wave_index.reshape(-1), axis=3)
    picked = picked.reshape(field_count, row_count, 2, lat_size, fld_size, slot_count)
    outgoing = jnp.transpose(picked, (5, 2, 4, 0, 3, 1)).reshape(
        slot_count, 2, fld_size * field_count, lat_size * row_count
    )
    received = lax.all_to_all(
        lax.all_to_all(outgoing, "lat", split_axis=3, concat_axis=3, tiled=True),
        "fld",
        split_axis=2,
        concat_axis=2,
        tiled=True,
    )
    group = lax.axis_index("lat") * fld_size + lax.axis_index("fld")
    own_waves = lax.dynamic_index_in_dim(waves, group, 0, keepdims=False)
    counts = jnp.where(own_waves >= 0, M - own_waves, 0)
    offsets = jnp.cumsum(counts) - counts
    col_count = legendre.shape[2]
    col_ids = lax.broadcasted_iota(jnp.int32, (slot_count, col_count), 1)
    segments = ((col_ids >= offsets[:, None]) & (col_ids < (offsets + counts)[:, None])).astype(
        jnp.float32
    )
    total_fields = fld_size * field_count
    regrouped = lax.all_to_all(received, "rep", split_axis=2, concat_axis=3, tiled=True)
    half_fields = total_fields // rep_size
    ordered = regrouped.reshape(slot_count, 2, half_fields, rep_size, lat_size, row_count)
    ordered = jnp.transpose(ordered, (0, 1, 2, 4, 3, 5)).reshape(
        slot_count * 2 * half_fields, rep_size * lat_size * row_count
    )
    products = jnp.dot(ordered, legendre[0], preferred_element_type=jnp.float32)
    spectrum = jnp.einsum(
        "scfk,sk->fck", products.reshape(slot_count, 2, half_fields, col_count), segments
    )
    return spectrum[None]


def solution(mesh):
    placed = (
        P("fld", ("lat", "rep"), None),
        P("fld", ("lat", "rep"), None),
        P("fld", ("lat", "rep"), None),
        P(),
        P(),
        P(("lat", "fld"), None, None),
    )
    return jax.shard_map(
        body,
        mesh=mesh,
        in_specs=placed,
        out_specs=P(("lat", "fld"), "rep", None, None),
        check_vma=False,
    )
```

```python
import functools
import math

import jax
import jax.numpy as jnp
from jax import lax
from jax.experimental import pallas as pl
from jax.experimental.pallas import tpu as pltpu
from jax.sharding import PartitionSpec as P

M = 1280
LANES = 128
WINDOW = 16
TILE = 4096
PAD = 8
CHUNK = 16


def with_halo(value, sides, width):
    for axis, dim in sides:
        peers, length = (lax.axis_size(axis), value.shape[dim])
        up = [(i, (i + 1) % peers) for i in range(peers - 1)]
        down = [(j, i) for i, j in up]
        last = lax.slice_in_dim(value, length - width, length, axis=dim)
        first = lax.slice_in_dim(value, 0, width, axis=dim)
        before = lax.ppermute(last, axis, up)
        after = lax.ppermute(first, axis, down)
        value = jnp.concatenate([before, value, after], axis=dim)
    return value


def dft_matrix(lon_count, wave_count):
    lon_ids = lax.broadcasted_iota(jnp.int32, (lon_count, wave_count), 0)
    wave_ids = lax.broadcasted_iota(jnp.int32, (lon_count, wave_count), 1)
    angles = (lon_ids * wave_ids % lon_count).astype(jnp.float32) * (2.0 * math.pi / lon_count)
    scaling = 1.0 / math.sqrt(lon_count)
    return jnp.concatenate([jnp.cos(angles) * scaling, -jnp.sin(angles) * scaling], axis=1).astype(
        jnp.bfloat16
    )


def tendency(centre, above_row, below_row, zonal_wind, merid_wind):
    eastward = jnp.roll(centre, -1, axis=-1)
    westward = jnp.roll(centre, 1, axis=-1)
    return (
        -(zonal_wind + centre) * (eastward - westward) * 0.5
        - merid_wind * (above_row - below_row) * 0.5
    )


def band_mask(bounds, first_row, row_total):
    row_ids = first_row + lax.broadcasted_iota(jnp.int32, (1, row_total, 1), 1)
    lower_edge = bounds[:, 0][:, None, None]
    upper_edge = bounds[:, 1][:, None, None]
    return ((row_ids >= lower_edge) & (row_ids < upper_edge)).astype(jnp.float32)


def transform_kernel(lon_count, table_ref, grid_ref, out_ref, matrix):
    slots = table_ref.shape[1]
    low_cos, low_sin = table_ref[0], table_ref[1]
    high_cos, high_sin = table_ref[2], table_ref[3]
    for part in range(lon_count // LANES):
        columns = slice(part * LANES, (part + 1) * LANES)
        scaled_cos = high_cos[:, part : part + 1]
        scaled_sin = high_sin[:, part : part + 1]
        matrix[0:slots, columns] = (scaled_cos * low_cos - scaled_sin * low_sin).astype(jnp.bfloat16)
        matrix[slots : 2 * slots, columns] = (-(scaled_sin * low_cos + scaled_cos * low_sin)).astype(
            jnp.bfloat16
        )
    out_ref[...] = lax.dot_general(
        matrix[...], grid_ref[...], (((1,), (1,)), ((), ())), preferred_element_type=jnp.float32
    ).astype(jnp.bfloat16)


def transform(grid_low, waves, lon_count):
    groups, slots = waves.shape
    wave_column = jnp.where(waves >= 0, waves, 0).reshape(1, groups * slots, 1)
    step = jnp.arange(2, dtype=jnp.int32).reshape(2, 1, 1) * (LANES - 1) + 1
    lane = lax.broadcasted_iota(jnp.int32, (1, 1, LANES), 2)
    turns = (wave_column * ((step * lane) % lon_count)) % lon_count
    angles = turns.astype(jnp.float32) * (2.0 * math.pi / lon_count)
    scale = jnp.array([1.0, 1.0 / math.sqrt(lon_count)], jnp.float32).reshape(2, 1, 1)
    tables = jnp.stack([jnp.cos(angles) * scale, jnp.sin(angles) * scale], axis=1)
    tables = tables.reshape(4, groups * slots, LANES)
    rows = grid_low.shape[0]
    return pl.pallas_call(
        functools.partial(transform_kernel, lon_count),
        out_shape=jax.ShapeDtypeStruct((groups * 2 * slots, rows), jnp.bfloat16),
        grid=(groups,),
        in_specs=[
            pl.BlockSpec((4, slots, LANES), lambda g: (0, g, 0)),
            pl.BlockSpec((rows, lon_count), lambda g: (0, 0)),
        ],
        out_specs=pl.BlockSpec((2 * slots, rows), lambda g: (g, 0)),
        scratch_shapes=[pltpu.VMEM((2 * slots, lon_count), jnp.bfloat16)],
        compiler_params=pltpu.CompilerParams(vmem_limit_bytes=32 << 20),
    )(tables, grid_low)


def exchange_kernel(lat_size, fld_size, rep_size, source, target, send_sem, recv_sem, own_sem):
    lat, fld, rep = lax.axis_index("lat"), lax.axis_index("fld"), lax.axis_index("rep")
    groups = lat_size * fld_size
    rows = target.shape[1]
    half = fld_size // rep_size
    to_rep = fld // half
    place = ((fld % half) * lat_size + lat) * rep_size + rep
    own = lat * fld_size + fld
    stays = to_rep == rep

    def sending(hop):
        group = (own + hop) % groups
        return pltpu.make_async_remote_copy(
            src_ref=source.at[pl.ds(pl.multiple_of(group * rows, 16), rows)],
            dst_ref=target.at[place],
            send_sem=send_sem.at[hop],
            recv_sem=recv_sem.at[place],
            device_id=(group // fld_size, group % fld_size, to_rep),
            device_id_type=pl.DeviceIdType.MESH,
        )

    kept = pltpu.make_async_copy(
        source.at[pl.ds(pl.multiple_of(own * rows, 16), rows)], target.at[place], own_sem
    )
    for hop in range(1, groups):
        sending(hop).start()

    @pl.when(stays)
    def _():
        kept.start()

    @pl.when(jnp.logical_not(stays))
    def _():
        sending(0).start()

    @pl.when(stays)
    def _():
        kept.wait()

    @pl.when(jnp.logical_not(stays))
    def _():
        sending(0).wait_send()

    for hop in range(1, groups):
        sending(hop).wait_send()
    for origin in range(target.shape[0]):

        @pl.when(jnp.logical_not(stays & (place == origin)))
        def _():
            pltpu.make_async_remote_copy(
                src_ref=target.at[origin],
                dst_ref=target.at[origin],
                send_sem=send_sem.at[0],
                recv_sem=recv_sem.at[origin],
                device_id=(lat, fld, 1 - rep),
                device_id_type=pl.DeviceIdType.MESH,
            ).wait_recv()


def exchange(spectra, lat_size, fld_size, rep_size):
    rows = spectra.shape[0] // (lat_size * fld_size)
    origins = fld_size // rep_size * lat_size * rep_size
    return pl.pallas_call(
        functools.partial(exchange_kernel, lat_size, fld_size, rep_size),
        out_shape=jax.ShapeDtypeStruct((origins, rows, spectra.shape[1]), spectra.dtype),
        in_specs=[pl.BlockSpec(memory_space=pltpu.VMEM)],
        out_specs=pl.BlockSpec(memory_space=pltpu.VMEM),
        scratch_shapes=[
            pltpu.SemaphoreType.DMA((lat_size * fld_size,)),
            pltpu.SemaphoreType.DMA((origins,)),
            pltpu.SemaphoreType.DMA,
        ],
        compiler_params=pltpu.CompilerParams(has_side_effects=True, vmem_limit_bytes=16 << 20),
    )(spectra)


def legendre_kernel(
    bands, field_count, first, last, received, starts, stops, legendre, out, ordered, total
):
    slots = starts.shape[0]
    row_count = received.shape[2] // field_count
    tile = pl.program_id(0)
    width = out.shape[3]

    @pl.when(tile == 0)
    def _():
        for origin in range(received.shape[0]):
            part, band = divmod(origin, bands)
            for level in range(field_count):
                for side in range(2):
                    row = (part * field_count + level) * 2 + side
                    ordered[row, :, band * row_count : (band + 1) * row_count] = received[
                        origin,
                        side * slots : (side + 1) * slots,
                        level * row_count : (level + 1) * row_count,
                    ]

    total[...] = jnp.zeros_like(total)
    rows = ordered.shape[0]

    @pl.loop(first[tile], last[tile])
    def _(window):
        here = pl.ds(pl.multiple_of(window * WINDOW, WINDOW), WINDOW)
        products = jnp.dot(
            ordered[:, here, :].reshape(rows * WINDOW, ordered.shape[2]),
            legendre[0],
            preferred_element_type=jnp.float32,
        ).reshape(rows, WINDOW, width)
        columns = tile * width + lax.broadcasted_iota(jnp.int32, (WINDOW, width), 1)
        held = (columns >= starts[here, :]) & (columns < stops[here, :])
        total[...] += jnp.sum(jnp.where(held[None], products, 0.0), axis=1)

    for level in range(rows // 2):
        out[0, level] = total[2 * level : 2 * level + 2, :]


def legendre_sums(received, own_waves, legendre, field_count, bands, wave_total):
    slots = own_waves.shape[0]
    counts = jnp.where(own_waves >= 0, wave_total - own_waves, 0)
    lower = lax.broadcasted_iota(jnp.int32, (slots, slots), 1) <= lax.broadcasted_iota(
        jnp.int32, (slots, slots), 0
    )
    stops = jnp.sum(jnp.where(lower, counts[None, :], 0), axis=1)
    starts = stops - counts
    depth, col_count = legendre.shape[1:]
    width = min(TILE, col_count)
    tiles = pl.cdiv(col_count, width)
    edges = jnp.arange(tiles, dtype=jnp.int32)[:, None] * width
    first = jnp.sum((stops[None, :] <= edges).astype(jnp.int32), axis=1) // WINDOW
    begun = jnp.sum((starts[None, :] < edges + width).astype(jnp.int32), axis=1)
    last = (begun + WINDOW - 1) // WINDOW
    rows = received.shape[0] // bands * field_count * 2
    return pl.pallas_call(
        functools.partial(legendre_kernel, bands, field_count),
        out_shape=jax.ShapeDtypeStruct((1, rows // 2, 2, col_count), jnp.float32),
        grid_spec=pltpu.PrefetchScalarGridSpec(
            num_scalar_prefetch=2,
            grid=(tiles,),
            in_specs=[
                pl.BlockSpec(
                    received.shape, lambda t, *_: (0, 0, 0), pipeline_mode=pl.Buffered(1)
                ),
                pl.BlockSpec((slots, 1), lambda t, *_: (0, 0)),
                pl.BlockSpec((slots, 1), lambda t, *_: (0, 0)),
                pl.BlockSpec((1, depth, width), lambda t, *_: (0, 0, t)),
            ],
            out_specs=pl.BlockSpec((1, rows // 2, 2, width), lambda t, *_: (0, 0, 0, t)),
            scratch_shapes=[
                pltpu.VMEM((rows, slots, depth), jnp.bfloat16),
                pltpu.VMEM((rows, width), jnp.float32),
            ],
        ),
        compiler_params=pltpu.CompilerParams(vmem_limit_bytes=56 << 20),
    )(first, last, received, starts[:, None], stops[:, None], legendre)


def advection_kernel(bounds, origin, field, zonal, merid, above, below, out, edges, padded, section):
    level = pl.program_id(0)
    rows = field.shape[1]
    length = field.shape[2]
    lower, upper, start = bounds[level, 0], bounds[level, 1], origin[0]

    def masked_slope(first_row, centre, turned_east, turned_west, next_row, previous, zonal_wind, merid_wind):
        row_ids = start + first_row + lax.broadcasted_iota(jnp.int32, centre.shape, 0)
        in_band = ((row_ids >= lower) & (row_ids < upper)).astype(jnp.float32)
        return in_band * (
            -(zonal_wind + centre) * (turned_east - turned_west) * 0.5
            - merid_wind * (next_row - previous) * 0.5
        )

    def turned(value):
        return pltpu.roll(value, length - 1, axis=1), pltpu.roll(value, 1, axis=1)

    padded[PAD : PAD + rows, :] = field[0]
    padded[PAD - 2 : PAD, :] = above[0, 0:2, :]
    padded[PAD + rows : PAD + rows + 2, :] = below[0, 0:2, :]
    edges[0:4, :] = above[0]
    edges[4:8, :] = below[0]
    halo = edges[...]
    east, west = turned(halo)
    section[PAD - 1 : PAD, :] = halo[1:2] + masked_slope(
        -1, halo[1:2], east[1:2], west[1:2], field[0, 0:1, :], halo[0:1], halo[2:3], halo[3:4]
    )
    section[PAD + rows : PAD + rows + 1, :] = halo[4:5] + masked_slope(
        rows, halo[4:5], east[4:5], west[4:5], halo[5:6], field[0, rows - 1 : rows, :], halo[6:7], halo[7:8]
    )

    def neighbours(ref, first_row):
        value = ref[pl.ds(first_row, 2 * PAD + CHUNK), :]
        return tuple(value[PAD + shift : PAD + shift + CHUNK] for shift in (-1, 0, 1))

    @pl.loop(0, rows // CHUNK)
    def _(chunk):
        first_row = pl.multiple_of(chunk * CHUNK, CHUNK)
        here = pl.ds(first_row, CHUNK)
        previous, centre, next_row = neighbours(padded, first_row)
        section[pl.ds(pl.multiple_of(first_row + PAD, PAD), CHUNK), :] = centre + masked_slope(
            first_row, centre, *turned(centre), next_row, previous, zonal[0, here, :], merid[0, here, :]
        )

    @pl.loop(0, rows // CHUNK)
    def _(chunk):
        first_row = pl.multiple_of(chunk * CHUNK, CHUNK)
        here = pl.ds(first_row, CHUNK)
        previous, centre, next_row = neighbours(section, first_row)
        out[0, here, :] = (
            0.5
            * (
                field[0, here, :]
                + centre
                + masked_slope(
                    first_row, centre, *turned(centre), next_row, previous, zonal[0, here, :], merid[0, here, :]
                )
            )
        ).astype(jnp.bfloat16)


def advection(field, wind_zonal, wind_merid, bounds, first_row):
    levels, rows, length = field.shape
    peers = lax.axis_size(("lat", "rep"))
    up = [(i, i + 1) for i in range(peers - 1)]
    down = [(i + 1, i) for i in range(peers - 1)]
    winds = (wind_zonal, wind_merid)
    above = lax.ppermute(
        jnp.concatenate([field[:, -2:]] + [w[:, -1:] for w in winds], axis=1), ("lat", "rep"), up
    )
    below = lax.ppermute(
        jnp.concatenate([field[:, :2]] + [w[:, :1] for w in winds], axis=1), ("lat", "rep"), down
    )
    whole = pl.BlockSpec((1, rows, length), lambda f, *_: (f, 0, 0))
    edge = pl.BlockSpec((1, 4, length), lambda f, *_: (f, 0, 0))
    return pl.pallas_call(
        advection_kernel,
        out_shape=jax.ShapeDtypeStruct(field.shape, jnp.bfloat16),
        grid_spec=pltpu.PrefetchScalarGridSpec(
            num_scalar_prefetch=2,
            grid=(levels,),
            in_specs=[whole, whole, whole, edge, edge],
            out_specs=whole,
            scratch_shapes=[
                pltpu.VMEM((8, length), jnp.float32),
                pltpu.VMEM((rows + 2 * PAD, length), jnp.float32),
                pltpu.VMEM((rows + 2 * PAD, length), jnp.float32),
            ],
        ),
        compiler_params=pltpu.CompilerParams(vmem_limit_bytes=60 << 20),
    )(bounds, first_row.reshape(1), field, wind_zonal, wind_merid, above, below)


def body(field, wind_zonal, wind_merid, band, waves, legendre):
    field_count, row_count, lon_count = field.shape
    lat_size = lax.axis_size("lat")
    fld_size = lax.axis_size("fld")
    rep_size = lax.axis_size("rep")
    first_row = (lax.axis_index("lat") * rep_size + lax.axis_index("rep")) * row_count
    bounds = lax.dynamic_slice_in_dim(band, lax.axis_index("fld") * field_count, field_count, 0)
    slot_count = waves.shape[1]
    direct = (
        row_count % 16 == 0
        and slot_count % WINDOW == 0
        and lon_count % LANES == 0
        and lon_count // LANES <= LANES
        and fld_size % rep_size == 0
        and lat_size * fld_size <= 64
    )
    if direct:
        grid_low = advection(field, wind_zonal, wind_merid, bounds, first_row)
        spectra = transform(
            grid_low.reshape(field_count * row_count, lon_count), waves, lon_count
        )
        received = exchange(spectra, lat_size, fld_size, rep_size)
        group = lax.axis_index("lat") * fld_size + lax.axis_index("fld")
        own_waves = lax.dynamic_index_in_dim(waves, group, 0, keepdims=False)
        return legendre_sums(
            received, own_waves, legendre, field_count, lat_size * rep_size, M
        )
    in_band = band_mask(bounds, first_row, row_count)
    padded = with_halo(field, ((("lat", "rep"), 1),), 1)
    first_section = field + in_band * tendency(
        field, padded[:, 2:], padded[:, :-2], wind_zonal, wind_merid
    )
    padded_section = with_halo(first_section, ((("lat", "rep"), 1),), 1)
    advected = 0.5 * (
        field
        + first_section
        + in_band
        * tendency(
            first_section, padded_section[:, 2:], padded_section[:, :-2], wind_zonal, wind_merid
        )
    )
    grid_low = advected.astype(jnp.bfloat16)
    spectra = jnp.dot(
        grid_low.reshape(field_count * row_count, lon_count),
        dft_matrix(lon_count, M),
        preferred_element_type=jnp.float32,
    ).astype(jnp.bfloat16)
    spectra = spectra.reshape(field_count, row_count, 2, M)
    wave_index = jnp.where(waves >= 0, waves, 0)
    picked = jnp.take(spectra, wave_index.reshape(-1), axis=3)
    picked = picked.reshape(field_count, row_count, 2, lat_size, fld_size, slot_count)
    outgoing = jnp.transpose(picked, (5, 2, 4, 0, 3, 1)).reshape(
        slot_count, 2, fld_size * field_count, lat_size * row_count
    )
    received = lax.all_to_all(
        lax.all_to_all(outgoing, "lat", split_axis=3, concat_axis=3, tiled=True),
        "fld",
        split_axis=2,
        concat_axis=2,
        tiled=True,
    )
    group = lax.axis_index("lat") * fld_size + lax.axis_index("fld")
    own_waves = lax.dynamic_index_in_dim(waves, group, 0, keepdims=False)
    counts = jnp.where(own_waves >= 0, M - own_waves, 0)
    offsets = jnp.cumsum(counts) - counts
    col_count = legendre.shape[2]
    col_ids = lax.broadcasted_iota(jnp.int32, (slot_count, col_count), 1)
    segments = ((col_ids >= offsets[:, None]) & (col_ids < (offsets + counts)[:, None])).astype(
        jnp.float32
    )
    total_fields = fld_size * field_count
    regrouped = lax.all_to_all(received, "rep", split_axis=2, concat_axis=3, tiled=True)
    half_fields = total_fields // rep_size
    ordered = regrouped.reshape(slot_count, 2, half_fields, rep_size, lat_size, row_count)
    ordered = jnp.transpose(ordered, (0, 1, 2, 4, 3, 5)).reshape(
        slot_count * 2 * half_fields, rep_size * lat_size * row_count
    )
    products = jnp.dot(ordered, legendre[0], preferred_element_type=jnp.float32)
    spectrum = jnp.einsum(
        "scfk,sk->fck", products.reshape(slot_count, 2, half_fields, col_count), segments
    )
    return spectrum[None]


def solution(mesh):
    placed = (
        P("fld", ("lat", "rep"), None),
        P("fld", ("lat", "rep"), None),
        P("fld", ("lat", "rep"), None),
        P(),
        P(),
        P(("lat", "fld"), None, None),
    )
    return jax.shard_map(
        body,
        mesh=mesh,
        in_specs=placed,
        out_specs=P(("lat", "fld"), "rep", None, None),
        check_vma=False,
    )
```
